32 devices in a mesh: inst: 4 (over z), mesh: 8 (over y, x, core).
Axes of the slice: x: 2, y: 2, z: 4, core: 2. Of those that a mesh axis runs over, the one named last changes fastest.
Arguments:
- state: float32 [16, 6, 512, 128], P('inst', None, 'mesh'), may hold values from -6 to 6
- right_side: float32 [16, 6, 512, 128], P('inst', None, 'mesh'), may hold values from -6 to 6
- couplings: float32 [3, 16, 6, 512, 128], P(None, 'inst', None, 'mesh'), may hold values from 0.05 to 0.35
- jac_corr: float32 [16, 6, 6, 512, 128], P('inst', None, None, 'mesh'), may hold values from -0.3 to 0.3
- spec_scale: float32 [512, 128], P('mesh'), may hold values from 0.005 to 0.05
- row_id: int32 [512], P('mesh'), may hold values from 0 to 2
- send_index: int32 [64, 2], P('mesh'), may hold values from 0 to 63
- recv_slot: int32 [512], P('mesh'), may hold values from 0 to 15, as said below
- iface_coef: float32 [16, 128], P('mesh'), may hold values from 0.2 to 0.6
- donor_index: int32 [16, 2], P('mesh'), may hold values from 0 to 15
- donor_weight: float32 [16, 2], P('mesh'), may hold values from 0.2 to 1
- phase_shift: int32 [16], P('mesh'), may hold values from 0 to 15
Outputs:
- smoothed: float32 [16, 6, 512, 128], P('inst', None, 'mesh')
The draws below stay inside these ranges and needn't reach their ends.
Inputs may be any that keep to these rules, and one draw needn't show every extreme that they name: `recv_slot`: among the 64 blocks of each mesh index, every slot 0 to 8 * 2 - 1 is named by at least one block.
All inputs are finite; a program needn't handle non-finite values.
Results may differ from the reference program's by a relative error of at most 0.0001.
Values sent between devices are 32-bit elements; how exact they have to be, the bound alone decides.
A program may use at most 64 MiB of HBM per device.

```python
import math
import jax
import jax.numpy as jnp
from jax import lax

NT = 16
NV = 6
BLOCK_CELLS = 128
BLK_DEV = 64
HALO_SLOTS = 2
IF_DEV = 2
SWEEPS = 2
NB = 512
IFACE = 16
N_MESH = 8


def draw_recv_slot(key, part):
    device_keys = jax.random.split(jax.random.fold_in(key, 7), N_MESH)

    def one_device(device_key):
        order = jax.random.permutation(device_key, jnp.arange(BLK_DEV, dtype=jnp.int32))
        return (order % (N_MESH * HALO_SLOTS)).astype(jnp.int32)
    return jax.vmap(one_device)(device_keys).reshape(-1).astype(jnp.int32)


def draw_donor_index(key, part):
    picks = jax.random.randint(jax.random.fold_in(key, 11), (IFACE, 2), 0, IFACE).astype(jnp.int32)
    picks = picks.at[0, 0].set(0)
    return picks.at[0, 1].set(N_MESH // 2 * IF_DEV).astype(jnp.int32)


def draw_phase_shift(key, part):
    shifts = jax.random.randint(jax.random.fold_in(key, 13), (IFACE,), 0, NT).astype(jnp.int32)
    return shifts.at[0].set(NT // 2).astype(jnp.int32)


def place_ends(entries, key, least, high):
    index_at = [jax.random.randint(jax.random.fold_in(key, axis), (), 0, length) for axis, length in enumerate(entries.shape)]
    widest = entries.shape.index(max(entries.shape))
    next_to = index_at[:widest] + [(index_at[widest] + 1) % entries.shape[widest]] + index_at[widest + 1:]
    return entries.at[tuple(index_at)].set(least).at[tuple(next_to)].set(high)


def levels(own_key, dims, cuts, least, high):
    level = 1.0
    for position, parts in cuts:
        draws = jax.random.uniform(jax.random.fold_in(jax.random.fold_in(own_key, 6), position), (parts,), jnp.float32, least / len(cuts), high / len(cuts))
        level = level * jnp.repeat(jnp.exp(draws), dims[position] // parts).reshape((-1,) + (1,) * (len(dims) - 1 - position))
    return level


def normal_values(rng, shape, scale, most, cuts=(), kind=jnp.bfloat16):
    level = levels(rng, shape, cuts, -0.22, 0.18) if cuts else 1.0
    drawn = jax.random.normal(rng, shape, jnp.float32) * scale * level
    return jnp.minimum(jnp.maximum(drawn, -most), most).astype(kind)


def setup_inputs(seed: int = 0) -> dict:
    splits = jax.random.split(jax.random.key(seed), 13)
    state = normal_values(splits[0], (NT, NV, NB, BLOCK_CELLS), 1.0, 6.0, ((0, 4), (2, 8)), jnp.float32)
    right_side = normal_values(splits[1], (NT, NV, NB, BLOCK_CELLS), 1.0, 6.0, ((0, 4), (2, 8)), jnp.float32)
    couplings = jnp.clip(0.05 + 0.29999999 * jax.random.uniform(splits[2], (3, NT, NV, NB, BLOCK_CELLS), jnp.float32) ** levels(splits[2], (3, NT, NV, NB, BLOCK_CELLS), ((1, 4), (3, 8)), -0.2, 0.2), 0.05, 0.35)
    jac_corr = normal_values(splits[3], (NT, NV, NV, NB, BLOCK_CELLS), 0.06, 0.3, ((0, 4), (3, 8)), jnp.float32)
    spec_scale = jnp.clip(jnp.exp(math.log(0.05) - 2.3025851 * jax.random.uniform(splits[4], (NB, BLOCK_CELLS), jnp.float32) ** levels(splits[4], (NB, BLOCK_CELLS), ((0, 8),), -0.2, 0.2)), 0.005, 0.05)
    row_id = place_ends(jax.random.randint(splits[5], (NB,), 0, 3), jax.random.fold_in(splits[5], 1), 0, 2).astype(jnp.int32)
    send_index = place_ends(jax.random.randint(splits[6], (N_MESH * N_MESH, HALO_SLOTS), 0, BLK_DEV), jax.random.fold_in(splits[6], 1), 0, BLK_DEV - 1).astype(jnp.int32)
    recv_slot = draw_recv_slot(jax.random.fold_in(splits[12], 71), 0)
    iface_coef = jnp.clip(0.2 + 0.400000021 * jax.random.uniform(splits[8], (IFACE, BLOCK_CELLS), jnp.float32) ** levels(splits[8], (IFACE, BLOCK_CELLS), ((0, 8),), -0.2, 0.2), 0.2, 0.6)
    donor_index = draw_donor_index(jax.random.fold_in(splits[12], 71), 0)
    donor_weight = jnp.clip(0.2 + 0.8 * jax.random.uniform(splits[10], (IFACE, 2), jnp.float32) ** levels(splits[10], (IFACE, 2), ((0, 8),), -0.2, 0.2), 0.2, 1.0)
    phase_shift = draw_phase_shift(jax.random.fold_in(splits[12], 71), 0)
    return dict(state=state, right_side=right_side, couplings=couplings, jac_corr=jac_corr, spec_scale=spec_scale, row_id=row_id, send_index=send_index, recv_slot=recv_slot, iface_coef=iface_coef, donor_index=donor_index, donor_weight=donor_weight, phase_shift=phase_shift)


def spectral_table(length):
    row_ids = jnp.arange(length)[:, None]
    col_ids = jnp.arange(length)[None, :]
    offsets = row_ids - col_ids
    parity = 1.0 - 2.0 * (offsets % 2).astype(jnp.float32)
    angles = jnp.pi * offsets.astype(jnp.float32) / length
    on_diag = offsets == 0
    sine_safe = jnp.where(on_diag, 1.0, jnp.sin(angles))
    first = jnp.where(on_diag, 0.0, 0.5 * parity * jnp.cos(angles) / sine_safe)
    diag_value = -(length * length + 2.0) / 12.0
    second = jnp.where(on_diag, diag_value, -0.5 * parity / (sine_safe * sine_safe))
    return first - 0.1 * second


def line_terms(field, couplings):
    zeros_col = jnp.zeros_like(field[..., :1])
    below = jnp.concatenate([zeros_col, field[..., :-1]], axis=-1)
    above = jnp.concatenate([field[..., 1:], zeros_col], axis=-1)
    return couplings[0] * below + couplings[1] * above


def jacobi_update(total_rhs, jac_corr):
    updated = 0.35 * total_rhs + jnp.einsum("nvwbc,nwbc->nvbc", jac_corr, total_rhs, precision=lax.Precision.HIGHEST)
    return updated.at[:, -1].set(jnp.maximum(updated[:, -1], 0.0))


def donor_mix(donor_pool, donor_index, donor_weight):
    first_part = donor_pool[:, :, donor_index[:, 0]] * donor_weight[:, 0][:, None]
    second_part = donor_pool[:, :, donor_index[:, 1]] * donor_weight[:, 1][:, None]
    return first_part + second_part


def phase_pick(combined, shift_src):
    targets = jnp.arange(combined.shape[2])[None, :]
    picked = combined[shift_src, :, targets]
    return jnp.transpose(picked, (0, 2, 1, 3))


def reference(state, right_side, couplings, jac_corr, spec_scale, row_id, send_index, recv_slot, iface_coef, donor_index, donor_weight, phase_shift):
    table = spectral_table(NT)
    owner = jnp.arange(NB) // BLK_DEV
    source_dev = recv_slot // HALO_SLOTS
    halo_block = source_dev * BLK_DEV + send_index[source_dev * N_MESH + owner, recv_slot % HALO_SLOTS]
    row_factor = 1.0 + 0.5 * row_id.astype(jnp.float32)
    frequency = spec_scale * row_factor[:, None]
    shift_src = (jnp.arange(NT)[:, None] + phase_shift[None, :]) % NT
    field = state
    for sweep_index in range(SWEEPS):
        spectral = jnp.einsum("nm,mvbc->nvbc", table, field, precision=lax.Precision.HIGHEST)
        halo_vals = field[:, :, halo_block]
        faces = field.reshape(NT, NV, N_MESH, BLK_DEV, BLOCK_CELLS)[:, :, :, :IF_DEV].reshape(NT, NV, IFACE, BLOCK_CELLS)
        combined = donor_mix(faces, donor_index, donor_weight)
        iface_term = iface_coef * phase_pick(combined, shift_src)
        total_rhs = right_side + line_terms(field, couplings) + couplings[2] * halo_vals - frequency * spectral
        total_rhs = total_rhs.reshape(NT, NV, N_MESH, BLK_DEV, BLOCK_CELLS)
        total_rhs = total_rhs.at[:, :, :, :IF_DEV].add(iface_term.reshape(NT, NV, N_MESH, IF_DEV, BLOCK_CELLS))
        total_rhs = total_rhs.reshape(NT, NV, NB, BLOCK_CELLS)
        field = jacobi_update(total_rhs, jac_corr)
    return field
```

```python
import functools

import jax
import jax.numpy as jnp
import numpy as np
from jax import lax
from jax.experimental import pallas as pl
from jax.experimental.pallas import tpu as pltpu
from jax.sharding import PartitionSpec as P

SWEEPS = 2
ROWS = 8
AHEAD = 3
FORWARD = 3
VMEM_LIMIT = 40 * 2**20
MESH_ID = pl.DeviceIdType.MESH


def spectral_matrix(length):
    offsets = np.arange(length)[:, None] - np.arange(length)[None, :]
    parity = 1.0 - 2.0 * (offsets % 2)
    angles = np.pi * offsets / length
    on_diag = offsets == 0
    sine = np.where(on_diag, 1.0, np.sin(angles))
    first = np.where(on_diag, 0.0, 0.5 * parity * np.cos(angles) / sine)
    second = np.where(on_diag, -(length * length + 2.0) / 12.0, -0.5 * parity / (sine * sine))
    return (first - 0.1 * second).astype(np.float32)


def hub_tables(n_inst, local):
    half, total = n_inst // 2, n_inst * local
    matrix = spectral_matrix(total)
    coefs, rows_abs, place = [], [], []
    for side in range(2):
        low, high = list(range(half - 1)), list(range(half + 1, n_inst))
        devs = [half - 1] + low + [half] + high if side == 0 else [half] + high + [half - 1] + low
        cols = np.array([d * local + i for d in devs for i in range(local)])
        rows = cols[: half * local]
        coefs.append(matrix[rows][:, cols].reshape(-1))
        rows_abs.append(rows)
        inverse = np.zeros(total, np.int32)
        inverse[cols] = np.arange(total)
        place.append(inverse)
    return np.stack(coefs), np.stack(rows_abs).astype(np.int32), np.stack(place)


def kernel(
    n_inst, n_mesh, dims,
    coef_in, rows_in, place_in, row_in, send_in, recv_in, donor_in, weight_in, phase_in,
    state, right_side, couplings, jac_corr, scale_in, iface_in,
    out,
    coef, rows_abs, place, row_id, send_index, recv_slot, donor_index, donor_weight, phase_shift, spec_scale, iface_coef,
    field0, field1, rhs, coup, jac, freq, halo, specin, specout, raw_leaf, raw_other, iadd, iadd_out,
    inc0, inc1, hsend, pool0, pool1, fsend,
    load_sem, small_sem, s_leaf, r_leaf, s_other, r_other, s_spec, r_spec, s_iadd, r_iadd, s_halo, r_halo, s_face, r_face,
):
    local, nv, blocks, cells, n_if, slots = dims
    half = n_inst // 2
    leaves = half - 1
    total = n_inst * local
    chunks = blocks // ROWS
    mid = chunks // 2
    me, my = lax.axis_index("inst"), lax.axis_index("mesh")
    side = me // half
    hub, other_hub = half - 1 + side, half - side
    leaf_at = me - side * (half + 1)
    fields = (field0, field1, out)
    inc, pool = (inc0, inc1), (pool0, pool1)

    loads = [
        pltpu.make_async_copy(src, dst, load_sem.at[i])
        for i, (src, dst) in enumerate(
            ((state, field0), (right_side, rhs), (couplings, coup), (jac_corr, jac))
        )
    ]
    smalls = [
        pltpu.make_async_copy(src, dst, small_sem.at[i])
        for i, (src, dst) in enumerate(
            (
                (coef_in, coef), (rows_in, rows_abs), (place_in, place), (row_in, row_id), (send_in, send_index),
                (recv_in, recv_slot), (donor_in, donor_index), (weight_in, donor_weight), (phase_in, phase_shift),
                (scale_in, spec_scale), (iface_in, iface_coef),
            )
        )
    ]
    loads[0].start()
    for copy in smalls:
        copy.start()

    barrier = pltpu.get_barrier_semaphore()
    for off in range(1, n_inst):
        pl.semaphore_signal(
            barrier, inc=1, device_id={"inst": lax.rem(me + off, n_inst)}, device_id_type=MESH_ID
        )
    for off in range(1, n_mesh):
        pl.semaphore_signal(
            barrier, inc=1, device_id={"mesh": lax.rem(my + off, n_mesh)}, device_id_type=MESH_ID
        )
    pl.semaphore_wait(barrier, n_inst + n_mesh - 2)

    first_order = list(range(chunks))
    second_order = list(range(1, mid + 1)) + [0] + list(range(mid + 1, chunks))
    seq = [(0, c) for c in first_order] + [(1, c) for c in second_order]

    def part(ref, c):
        return ref.at[:, :, pl.ds(c * ROWS, ROWS), :]

    def remote(src, dst, send, recv, axis, dev):
        return pltpu.make_async_remote_copy(
            src_ref=src, dst_ref=dst, send_sem=send, recv_sem=recv,
            device_id={axis: dev}, device_id_type=MESH_ID,
        )

    def leaf_copy(s, c, i):
        return remote(
            part(fields[s], c), part(raw_leaf.at[s, i], c), s_leaf.at[s, c], r_leaf.at[s, i, c], "inst", hub
        )

    def own_copy(s, c):
        return remote(
            part(fields[s], c), part(raw_other.at[s, 0], c),
            s_other.at[s, 0, c], r_other.at[s, 0, c], "inst", other_hub,
        )

    def forward_copy(s, c, i):
        return remote(
            part(raw_leaf.at[s, i], c), part(raw_other.at[s, i + 1], c),
            s_other.at[s, i + 1, c], r_other.at[s, i + 1, c], "inst", other_hub,
        )

    def spec_copy(s, c, i):
        return remote(
            part(specout.at[s, i], c), part(specin.at[s], c),
            s_spec.at[s, i, c], r_spec.at[s, c], "inst", i + side * (half + 1),
        )

    def iadd_copy(s, i):
        return remote(
            iadd_out.at[s, i], iadd.at[s], s_iadd.at[s, i], r_iadd.at[s], "inst", i + side * (half + 1)
        )

    def halo_copy(s, off):
        dev = lax.rem(my + off, n_mesh)
        return remote(hsend.at[s, dev], inc[s].at[my], s_halo.at[s, off], r_halo.at[s, off], "mesh", dev)

    def face_copy(s, off):
        dev = lax.rem(my + off, n_mesh)
        return remote(fsend.at[s], pool[s].at[my], s_face.at[s, off], r_face.at[s, off], "mesh", dev)

    def send_halo(s):
        def stage(d, carry):
            for k in range(slots):
                row = send_index[k, d]
                flat = fields[s].reshape(local * nv * blocks, cells)
                hsend[s, d, k] = flat[pl.ds(row, local * nv, stride=blocks), :]
            return carry

        lax.fori_loop(0, n_mesh, stage, 0)
        for off in range(1, n_mesh):
            halo_copy(s, off).start()
        for k in range(slots):
            inc[s][my, k] = hsend[s, my, k]

    def take_halo(s):
        for off in range(1, n_mesh):
            halo_copy(s, off).wait_recv()

    def expand_halo(s, c):
        flat = halo.reshape(local * nv * blocks, cells)
        for b in range(c * ROWS, c * ROWS + ROWS):
            slot = recv_slot[b]
            flat[pl.ds(b, local * nv, stride=blocks), :] = inc[s][slot // slots, slot % slots]

    def sources(s):
        refs = [(fields[s], n) for n in range(local)]
        refs += [(raw_leaf.at[s, i], n) for i in range(leaves) for n in range(local)]
        refs += [(raw_other.at[s, i], n) for i in range(half) for n in range(local)]
        return refs

    def spectral(s, row, v, rows):
        acc = None
        for col, (ref, n) in enumerate(sources(s)):
            term = coef[side, row * total + col] * ref[n, v, rows, :]
            acc = term if acc is None else acc + term
        return acc

    def update(s, c, is_hub):
        field, target = fields[s], fields[s + 1]
        rows = pl.ds(c * ROWS, ROWS)
        lane = lax.broadcasted_iota(jnp.int32, (ROWS, cells), 1)

        def one(n, carry):
            parts = []
            for v in range(nv):
                x = field[n, v, rows, :]
                below = jnp.where(lane == 0, 0.0, pltpu.roll(x, 1, 1))
                above = jnp.where(lane == cells - 1, 0.0, pltpu.roll(x, cells - 1, 1))
                spec = spectral(s, n, v, rows) if is_hub else specin[s, n, v, rows, :]
                value = rhs[n, v, rows, :] + coup[0, n, v, rows, :] * below + coup[1, n, v, rows, :] * above
                value = value + coup[2, n, v, rows, :] * halo[n, v, rows, :] - freq[rows, :] * spec
                if c == 0:
                    value = value + iadd[s, n, v]
                parts.append(value)
            for v in range(nv):
                acc = 0.35 * parts[v]
                for w in range(nv):
                    acc = acc + jac[n, v, w, rows, :] * parts[w]
                if v == nv - 1 and s + 1 < SWEEPS:
                    acc = jnp.maximum(acc, 0.0)
                target[n, v, rows, :] = acc
            return carry

        lax.fori_loop(0, local, one, 0)

    def send_faces(s):
        for col, (ref, n) in enumerate(sources(s)):
            for j in range(n_if):
                for v in range(nv):
                    fsend[s, j, col, pl.ds(v, 1), :] = ref[n, v, pl.ds(j, 1), :]
        for off in range(1, n_mesh):
            face_copy(s, off).start()
        for j in range(n_if):
            pool[s][my, j] = fsend[s, j]

    def mix_faces(s):
        for off in range(1, n_mesh):
            face_copy(s, off).wait_recv()
        for j in range(n_if):
            first, second = donor_index[j, 0], donor_index[j, 1]
            scale = iface_coef[pl.ds(j, 1), :]

            def one(row, carry):
                at = place[side, lax.rem(rows_abs[side, row] + phase_shift[j], total)]
                mixed = donor_weight[j, 0] * pool[s][first // n_if, first % n_if, at]
                mixed = mixed + donor_weight[j, 1] * pool[s][second // n_if, second % n_if, at]
                return mixed * scale

            for n in range(local):
                value = one(n, 0)
                for v in range(nv):
                    iadd[s, n, v, pl.ds(j, 1), :] = value[v : v + 1]
            for i in range(leaves):
                for n in range(local):
                    value = one((i + 1) * local + n, 0)
                    for v in range(nv):
                        iadd_out[s, i, n, v, pl.ds(j, 1), :] = value[v : v + 1]
        for i in range(leaves):
            iadd_copy(s, i).start()

    def prepare():
        for copy in loads[1:]:
            copy.wait()

        def one(b, carry):
            freq[pl.ds(b, 1), :] = spec_scale[pl.ds(b, 1), :] * (1.0 + 0.5 * row_id[b].astype(jnp.float32))
            return carry

        lax.fori_loop(0, blocks, one, 0)

    def run(is_hub):
        def get(s, c):
            if not is_hub:
                spec_copy(s, c, 0).wait_recv()
                return
            own_copy(s, c).wait_recv()
            for i in range(leaves):
                forward_copy(s, c, i).wait_recv()
            rows = pl.ds(c * ROWS, ROWS)
            for i in range(leaves):
                def one(n, carry, i=i):
                    for v in range(nv):
                        specout[s, i, n, v, rows, :] = spectral(s, (i + 1) * local + n, v, rows)
                    return carry

                lax.fori_loop(0, local, one, 0)
                spec_copy(s, c, i).start()
            if c == 0:
                send_faces(s)

        def forward(j):
            if is_hub and j < len(seq):
                for i in range(leaves):
                    leaf_copy(*seq[j], i).wait_recv()
                    forward_copy(*seq[j], i).start()

        def smooth(s, c):
            if c == 0:
                if is_hub:
                    mix_faces(s)
                else:
                    iadd_copy(s, 0).wait_recv()
            expand_halo(s, c)
            update(s, c, is_hub)
            if s + 1 < SWEEPS and not is_hub:
                leaf_copy(s + 1, c, leaf_at).start()

        if is_hub:
            for j in range(AHEAD):
                own_copy(*seq[j]).start()
            for s in range(SWEEPS):
                iadd[s] = jnp.zeros_like(iadd[s])
                iadd_out[s] = jnp.zeros_like(iadd_out[s])
        else:
            for c in first_order:
                leaf_copy(0, c, leaf_at).start()
        for copy in loads[1:]:
            copy.start()
        send_halo(0)
        for j in range(FORWARD):
            forward(j)
        pending = []
        for j, (s, c) in enumerate(seq):
            if is_hub and j + AHEAD < len(seq):
                own_copy(*seq[j + AHEAD]).start()
            forward(j + FORWARD)
            get(s, c)
            if s == 0:
                if j == 0:
                    prepare()
                    take_halo(0)
                if c > 0:
                    smooth(0, c)
                if j == mid:
                    smooth(0, 0)
                if j == chunks - 1:
                    send_halo(1)
            else:
                p = j - chunks
                if p == 2:
                    take_halo(1)
                if c > 0:
                    pending.append(c)
                if p == chunks - 2:
                    pending.append(0)
                for _ in range(2):
                    if p >= 2 and pending:
                        smooth(1, pending.pop(0))
        for c in pending:
            smooth(1, c)
        for s, c in seq:
            if is_hub:
                own_copy(s, c).wait_send()
                for i in range(leaves):
                    forward_copy(s, c, i).wait_send()
                    spec_copy(s, c, i).wait_send()
            else:
                leaf_copy(s, c, leaf_at).wait_send()
        for s in range(SWEEPS):
            for off in range(1, n_mesh):
                halo_copy(s, off).wait_send()
                if is_hub:
                    face_copy(s, off).wait_send()
            if is_hub:
                for i in range(leaves):
                    iadd_copy(s, i).wait_send()

    loads[0].wait()
    for copy in smalls:
        copy.wait()

    @pl.when(me == hub)
    def _():
        run(True)

    if leaves:
        @pl.when(me != hub)
        def _():
            run(False)


def per_device(
    n_inst, n_mesh,
    state, right_side, couplings, jac_corr, spec_scale, row_id, send_index, recv_slot,
    iface_coef, donor_index, donor_weight, phase_shift,
):
    local, nv, blocks, cells = state.shape
    n_if, slots = iface_coef.shape[0], send_index.shape[1]
    half, total = n_inst // 2, n_inst * local
    spare = max(half - 1, 1)
    chunks = blocks // ROWS
    tables = [jnp.asarray(t) for t in hub_tables(n_inst, local)]
    f32 = jnp.float32
    dma = pltpu.SemaphoreType.DMA
    whole = (local, nv, blocks, cells)
    add = (local, nv, ROWS, cells)
    vmem = lambda *shape: pltpu.VMEM(shape, f32)
    smem = lambda x: pltpu.SMEM(x.shape, x.dtype)
    smalls = [*tables, row_id, send_index.T, recv_slot, donor_index, donor_weight, phase_shift]
    call = pl.pallas_call(
        functools.partial(kernel, n_inst, n_mesh, (local, nv, blocks, cells, n_if, slots)),
        out_shape=pltpu.VMEM(whole, f32),
        in_specs=[pl.BlockSpec(memory_space=pltpu.HBM)] * 15,
        out_specs=pl.BlockSpec(memory_space=pltpu.VMEM),
        scratch_shapes=[
            *[smem(x) for x in smalls], vmem(blocks, cells), vmem(n_if, cells),
            vmem(*whole), vmem(*whole), vmem(*whole), vmem(3, *whole), vmem(local, nv, nv, blocks, cells),
            vmem(blocks, cells), vmem(*whole), vmem(SWEEPS, *whole), vmem(SWEEPS, spare, *whole),
            vmem(SWEEPS, spare, *whole), vmem(SWEEPS, half, *whole), vmem(SWEEPS, *add), vmem(SWEEPS, spare, *add),
            vmem(n_mesh, slots, local * nv, cells), vmem(n_mesh, slots, local * nv, cells),
            vmem(SWEEPS, n_mesh, slots, local * nv, cells),
            vmem(n_mesh, n_if, total, nv, cells), vmem(n_mesh, n_if, total, nv, cells),
            vmem(SWEEPS, n_if, total, nv, cells),
            dma((4,)), dma((11,)),
            dma((SWEEPS, chunks)), dma((SWEEPS, spare, chunks)),
            dma((SWEEPS, half, chunks)), dma((SWEEPS, half, chunks)),
            dma((SWEEPS, spare, chunks)), dma((SWEEPS, chunks)),
            dma((SWEEPS, spare)), dma((SWEEPS,)),
            dma((SWEEPS, n_mesh)), dma((SWEEPS, n_mesh)), dma((SWEEPS, n_mesh)), dma((SWEEPS, n_mesh)),
        ],
        compiler_params=pltpu.CompilerParams(
            collective_id=0, has_side_effects=True, vmem_limit_bytes=VMEM_LIMIT
        ),
        name="smooth",
    )
    operands = (*smalls, state, right_side, couplings, jac_corr, spec_scale, iface_coef)
    updated = call(*(pltpu.with_memory_space_constraint(x, pltpu.HBM) for x in operands))
    least = np.full((nv, 1, 1), -np.inf, np.float32)
    least[-1] = 0.0
    return jnp.maximum(updated, least)


def solution(mesh):
    return jax.shard_map(
        functools.partial(per_device, mesh.shape["inst"], mesh.shape["mesh"]),
        mesh=mesh,
        in_specs=(
            P("inst", None, "mesh", None),
            P("inst", None, "mesh", None),
            P(None, "inst", None, "mesh", None),
            P("inst", None, None, "mesh", None),
            P("mesh", None),
            P("mesh"),
            P("mesh", None),
            P("mesh"),
            P("mesh", None),
            P("mesh", None),
            P("mesh", None),
            P("mesh"),
        ),
        out_specs=P("inst", None, "mesh", None),
        check_vma=False,
    )
```

```python
import functools

import jax
import jax.numpy as jnp
import numpy as np
from jax import lax
from jax.experimental import pallas as pl
from jax.experimental.pallas import tpu as pltpu
from jax.sharding import PartitionSpec as P

SWEEPS = 2
ROWS = 8
AHEAD = 3
FORWARD = 3
LATE = 3
VMEM_LIMIT = 40 * 2**20
MESH_ID = pl.DeviceIdType.MESH


def spectral_matrix(length):
    offsets = np.arange(length)[:, None] - np.arange(length)[None, :]
    parity = 1.0 - 2.0 * (offsets % 2)
    angles = np.pi * offsets / length
    on_diag = offsets == 0
    sine = np.where(on_diag, 1.0, np.sin(angles))
    first = np.where(on_diag, 0.0, 0.5 * parity * np.cos(angles) / sine)
    second = np.where(on_diag, -(length * length + 2.0) / 12.0, -0.5 * parity / (sine * sine))
    return (first - 0.1 * second).astype(np.float32)


def hub_tables(n_inst, local):
    half, total = n_inst // 2, n_inst * local
    matrix = spectral_matrix(total)
    coefs, rows_abs, place = [], [], []
    for side in range(2):
        low, high = list(range(half - 1)), list(range(half + 1, n_inst))
        devs = [half - 1] + low + [half] + high if side == 0 else [half] + high + [half - 1] + low
        cols = np.array([d * local + i for d in devs for i in range(local)])
        rows = cols[: half * local]
        coefs.append(matrix[cols][:, cols].reshape(-1))
        rows_abs.append(rows)
        inverse = np.zeros(total, np.int32)
        inverse[cols] = np.arange(total)
        place.append(inverse)
    return np.stack(coefs), np.stack(rows_abs).astype(np.int32), np.stack(place)


def kernel(
    n_inst, n_mesh, dims,
    coef_in, rows_in, place_in, row_in, send_in, recv_in, donor_in, weight_in, phase_in,
    state, right_side, couplings, jac_corr, scale_in, iface_in,
    out,
    coef, rows_abs, place, row_id, send_index, recv_slot, donor_index, donor_weight, phase_shift, spec_scale, iface_coef,
    field0, field1, rhs, coup, jac, freq, halo, specin, specfar, specout, farout, raw_leaf, raw_other, iadd, iadd_out,
    inc0, inc1, hsend, pool0, pool1, fsend,
    load_sem, small_sem, s_leaf, r_leaf, s_other, r_other, s_spec, r_spec, s_iadd, r_iadd, s_halo, r_halo, s_face, r_face, s_far, r_far, ready,
):
    local, nv, blocks, cells, n_if, slots = dims
    half = n_inst // 2
    leaves = half - 1
    total = n_inst * local
    chunks = blocks // ROWS
    mid = chunks // 2
    me, my = lax.axis_index("inst"), lax.axis_index("mesh")
    side = me // half
    hub, other_hub = half - 1 + side, half - side
    leaf_at = me - side * (half + 1)
    fields, sent = (field0, field1, out), (state, field1)
    inc, pool = (inc0, inc1), (pool0, pool1)

    loads = [
        pltpu.make_async_copy(src, dst, load_sem.at[i])
        for i, (src, dst) in enumerate(
            ((state, field0), (right_side, rhs), (couplings, coup), (jac_corr, jac))
        )
    ]
    smalls = [
        pltpu.make_async_copy(src, dst, small_sem.at[i])
        for i, (src, dst) in enumerate(
            (
                (coef_in, coef), (rows_in, rows_abs), (place_in, place), (row_in, row_id), (send_in, send_index),
                (recv_in, recv_slot), (donor_in, donor_index), (weight_in, donor_weight), (phase_in, phase_shift),
                (scale_in, spec_scale), (iface_in, iface_coef),
            )
        )
    ]
    loads[0].start()
    for copy in smalls:
        copy.start()

    barrier = pltpu.get_barrier_semaphore()
    first_leaf = side * (half + 1)

    def greet(**where):
        pl.semaphore_signal(barrier, inc=1, device_id=where, device_id_type=MESH_ID)

    @pl.when(me == hub)
    def _():
        greet(inst=other_hub)
        for dev in range(n_mesh):
            greet(inst=first_leaf, mesh=dev)
        for i in range(1, leaves):
            greet(inst=first_leaf + i)

    @pl.when(me != hub)
    def _():
        for off in range(1, n_mesh):
            greet(mesh=lax.rem(my + off, n_mesh))

    greetings = jnp.where(leaf_at == 0, 2 * n_mesh - 1, n_mesh)
    pl.semaphore_wait(barrier, jnp.where(me == hub, 1, greetings))

    first_order = list(range(chunks))
    turn = min(LATE, chunks - 1)
    second_order = list(range(1, turn + 1)) + [0] + list(range(turn + 1, chunks))
    seq = [(0, c) for c in first_order] + [(1, c) for c in second_order]

    def part(ref, c):
        return ref.at[:, :, pl.ds(c * ROWS, ROWS), :]

    def remote(src, dst, send, recv, axis, dev):
        return pltpu.make_async_remote_copy(
            src_ref=src, dst_ref=dst, send_sem=send, recv_sem=recv,
            device_id={axis: dev}, device_id_type=MESH_ID,
        )

    def leaf_copy(s, c, i):
        return remote(
            part(sent[s], c), part(raw_leaf.at[s, i], c), s_leaf.at[s, c], r_leaf.at[s, i, c], "inst", hub
        )

    def own_copy(s, c):
        return remote(
            part(sent[s], c), part(raw_other.at[s, 0], c),
            s_other.at[s, 0, c], r_other.at[s, 0, c], "inst", other_hub,
        )

    def forward_copy(s, c, i):
        return remote(
            part(raw_leaf.at[s, i], c), part(raw_other.at[s, i + 1], c),
            s_other.at[s, i + 1, c], r_other.at[s, i + 1, c], "inst", other_hub,
        )

    def spec_copy(s, c, i):
        return remote(
            part(specout.at[s, i], c), part(specin.at[s], c),
            s_spec.at[s, i, c], r_spec.at[s, c], "inst", i + side * (half + 1),
        )

    def far_copy(c, k):
        dev = other_hub if k == 0 else k - 1 + (1 - side) * (half + 1)
        return remote(part(farout.at[k], c), part(specfar, c), s_far.at[k, c], r_far.at[c], "inst", dev)

    def iadd_copy(s, i):
        return remote(
            iadd_out.at[s, i], iadd.at[s], s_iadd.at[s, i], r_iadd.at[s], "inst", i + side * (half + 1)
        )

    def halo_copy(s, off):
        dev = lax.rem(my + off, n_mesh)
        return remote(hsend.at[s, dev], inc[s].at[my], s_halo.at[s, off], r_halo.at[s, off], "mesh", dev)

    def face_copy(s, off):
        dev = lax.rem(my + off, n_mesh)
        return remote(fsend.at[s], pool[s].at[my], s_face.at[s, off], r_face.at[s, off], "mesh", dev)

    def send_halo(s):
        def stage(d, carry):
            for k in range(slots):
                row = send_index[k, d]
                flat = fields[s].reshape(local * nv * blocks, cells)
                hsend[s, d, k] = flat[pl.ds(row, local * nv, stride=blocks), :]
            return carry

        lax.fori_loop(0, n_mesh, stage, 0)
        for off in range(1, n_mesh):
            halo_copy(s, off).start()
        for k in range(slots):
            inc[s][my, k] = hsend[s, my, k]

    def take_halo(s):
        for off in range(1, n_mesh):
            halo_copy(s, off).wait_recv()

    def expand_halo(s, c):
        flat = halo.reshape(local * nv * blocks, cells)
        for b in range(c * ROWS, c * ROWS + ROWS):
            slot = recv_slot[b]
            flat[pl.ds(b, local * nv, stride=blocks), :] = inc[s][slot // slots, slot % slots]

    def sources(s):
        refs = [(fields[s], n) for n in range(local)]
        refs += [(raw_leaf.at[s, i], n) for i in range(leaves) for n in range(local)]
        refs += [(raw_other.at[s, i], n) for i in range(half) for n in range(local)]
        return refs

    def spectral(s, row, v, rows, cols=total):
        acc = None
        for col, (ref, n) in enumerate(sources(s)[:cols]):
            term = coef[side, row * total + col] * ref[n, v, rows, :]
            acc = term if acc is None else acc + term
        return acc

    def update(s, c, is_hub, stage=None):
        field, target = fields[s], fields[s + 1]
        rows = pl.ds(c * ROWS, ROWS)
        lane = lax.broadcasted_iota(jnp.int32, (ROWS, cells), 1)

        def gather(n, v):
            if stage == 1:
                return rhs[n, v, rows, :] - freq[rows, :] * specfar[n, v, rows, :]
            x = field[n, v, rows, :]
            below = jnp.where(lane == 0, 0.0, pltpu.roll(x, 1, 1))
            above = jnp.where(lane == cells - 1, 0.0, pltpu.roll(x, cells - 1, 1))
            spec = spectral(s, n, v, rows) if is_hub and stage is None else specin[s, n, v, rows, :]
            value = rhs[n, v, rows, :] + coup[0, n, v, rows, :] * below + coup[1, n, v, rows, :] * above
            value = value + coup[2, n, v, rows, :] * halo[n, v, rows, :] - freq[rows, :] * spec
            if c == 0:
                value = value + iadd[s, n, v]
            return value

        def one(n, carry):
            if stage == 0:
                for v in range(nv):
                    rhs[n, v, rows, :] = gather(n, v)
                return carry
            parts = [gather(n, v) for v in range(nv)]
            for v in range(nv):
                acc = 0.35 * parts[v]
                for w in range(nv):
                    acc = acc + jac[n, v, w, rows, :] * parts[w]
                if v == nv - 1 and s + 1 < SWEEPS:
                    acc = jnp.maximum(acc, 0.0)
                target[n, v, rows, :] = acc
            return carry

        lax.fori_loop(0, local, one, 0)

    def send_faces(s):
        for col, (ref, n) in enumerate(sources(s)):
            for j in range(n_if):
                for v in range(nv):
                    fsend[s, j, col, pl.ds(v, 1), :] = ref[n, v, pl.ds(j, 1), :]
        for off in range(1, n_mesh):
            face_copy(s, off).start()
        for j in range(n_if):
            pool[s][my, j] = fsend[s, j]

    def mix_faces(s):
        for off in range(1, n_mesh):
            face_copy(s, off).wait_recv()
        for j in range(n_if):
            first, second = donor_index[j, 0], donor_index[j, 1]
            scale = iface_coef[pl.ds(j, 1), :]

            def one(row, carry):
                at = place[side, lax.rem(rows_abs[side, row] + phase_shift[j], total)]
                mixed = donor_weight[j, 0] * pool[s][first // n_if, first % n_if, at]
                mixed = mixed + donor_weight[j, 1] * pool[s][second // n_if, second % n_if, at]
                return mixed * scale

            for n in range(local):
                value = one(n, 0)
                for v in range(nv):
                    iadd[s, n, v, pl.ds(j, 1), :] = value[v : v + 1]
            for i in range(leaves):
                for n in range(local):
                    value = one((i + 1) * local + n, 0)
                    for v in range(nv):
                        iadd_out[s, i, n, v, pl.ds(j, 1), :] = value[v : v + 1]
        for i in range(leaves):
            iadd_copy(s, i).start()

    def prepare():
        for copy in loads[1:]:
            copy.wait()

        def one(b, carry):
            freq[pl.ds(b, 1), :] = spec_scale[pl.ds(b, 1), :] * (1.0 + 0.5 * row_id[b].astype(jnp.float32))
            return carry

        lax.fori_loop(0, blocks, one, 0)

    def run(is_hub):
        last = SWEEPS - 1

        def summed(s, c):
            return s == last and c > 0

        def get(s, c):
            if not is_hub:
                spec_copy(s, c, 0).wait_recv()
                return
            own_copy(s, c).wait_recv()
            for i in range(leaves):
                forward_copy(s, c, i).wait_recv()
            for i in range(leaves):
                sums(s, c, i + 1, total, specout.at[s, i])
                spec_copy(s, c, i).start()
            if c == 0:
                send_faces(s)

        def sums(s, c, block, cols, target):
            rows = pl.ds(c * ROWS, ROWS)

            def one(n, carry):
                for v in range(nv):
                    target[n, v, rows, :] = spectral(s, block * local + n, v, rows, cols)
                return carry

            lax.fori_loop(0, local, one, 0)

        def send_sums(c):
            cols = half * local
            for i in range(leaves):
                leaf_copy(last, c, i).wait_recv()
            for i in range(leaves):
                sums(last, c, half + 1 + i, cols, farout.at[i + 1])
                far_copy(c, i + 1).start()
            sums(last, c, half, cols, farout.at[0])
            far_copy(c, 0).start()
            for i in range(leaves):
                sums(last, c, i + 1, cols, specout.at[last, i])
                spec_copy(last, c, i).start()
            sums(last, c, 0, cols, specin.at[last])

        def own(j):
            if is_hub and j < len(seq) and not summed(*seq[j]):
                own_copy(*seq[j]).start()

        def forward(j):
            if not is_hub or j >= len(seq):
                return
            if summed(*seq[j]):
                send_sums(seq[j][1])
                return
            for i in range(leaves):
                leaf_copy(*seq[j], i).wait_recv()
                forward_copy(*seq[j], i).start()

        def smooth(s, c):
            if c == 0:
                if is_hub:
                    mix_faces(s)
                else:
                    iadd_copy(s, 0).wait_recv()
            expand_halo(s, c)
            update(s, c, is_hub)
            if s + 1 < SWEEPS and not is_hub:
                leaf_copy(s + 1, c, leaf_at).start()

        def finish(c):
            if not is_hub:
                spec_copy(last, c, 0).wait_recv()
            expand_halo(last, c)
            update(last, c, is_hub, 0)
            far_copy(c, 0).wait_recv()
            update(last, c, is_hub, 1)

        if is_hub:
            for j in range(AHEAD):
                own(j)
        else:
            pl.semaphore_signal(ready, inc=1, device_id={"inst": hub}, device_id_type=MESH_ID)
            for c in first_order:
                leaf_copy(0, c, leaf_at).start()
        for copy in loads[1:]:
            copy.start()
        loads[0].wait()
        for copy in smalls:
            copy.wait()
        if is_hub:
            for s in range(SWEEPS):
                iadd[s] = jnp.zeros_like(iadd[s])
                iadd_out[s] = jnp.zeros_like(iadd_out[s])
            pl.semaphore_wait(ready, leaves)
        send_halo(0)
        for j in range(FORWARD):
            forward(j)
        for j, c in enumerate(first_order):
            own(j + AHEAD)
            forward(j + FORWARD)
            get(0, c)
            if j == 0:
                prepare()
                take_halo(0)
            if c > 0:
                smooth(0, c)
            if j == mid:
                smooth(0, 0)
        send_halo(1)
        waiting = []
        for p, c in enumerate(second_order):
            own(chunks + p + AHEAD)
            forward(chunks + p + FORWARD)
            if c == 0:
                get(1, 0)
            else:
                waiting.append(c)
            if p == 2:
                take_halo(1)
            if p >= 2:
                for w in waiting:
                    finish(w)
                waiting = []
            if p == min(turn + 2, chunks - 1):
                smooth(1, 0)
        for s, c in seq:
            if is_hub:
                if summed(s, c):
                    for k in range(half):
                        far_copy(c, k).wait_send()
                else:
                    own_copy(s, c).wait_send()
                    for i in range(leaves):
                        forward_copy(s, c, i).wait_send()
                for i in range(leaves):
                    spec_copy(s, c, i).wait_send()
            else:
                leaf_copy(s, c, leaf_at).wait_send()
        for s in range(SWEEPS):
            for off in range(1, n_mesh):
                halo_copy(s, off).wait_send()
                if is_hub:
                    face_copy(s, off).wait_send()
            if is_hub:
                for i in range(leaves):
                    iadd_copy(s, i).wait_send()

    @pl.when(me == hub)
    def _():
        run(True)

    @pl.when(me != hub)
    def _():
        run(False)


def per_device(
    n_inst, n_mesh,
    state, right_side, couplings, jac_corr, spec_scale, row_id, send_index, recv_slot,
    iface_coef, donor_index, donor_weight, phase_shift,
):
    local, nv, blocks, cells = state.shape
    n_if, slots = iface_coef.shape[0], send_index.shape[1]
    half, total = n_inst // 2, n_inst * local
    spare = max(half - 1, 1)
    chunks = blocks // ROWS
    tables = [jnp.asarray(t) for t in hub_tables(n_inst, local)]
    f32 = jnp.float32
    dma = pltpu.SemaphoreType.DMA
    whole = (local, nv, blocks, cells)
    add = (local, nv, ROWS, cells)
    vmem = lambda *shape: pltpu.VMEM(shape, f32)
    smem = lambda x: pltpu.SMEM(x.shape, x.dtype)
    smalls = [*tables, row_id, send_index.T, recv_slot, donor_index, donor_weight, phase_shift]
    call = pl.pallas_call(
        functools.partial(kernel, n_inst, n_mesh, (local, nv, blocks, cells, n_if, slots)),
        out_shape=pltpu.VMEM(whole, f32),
        in_specs=[pl.BlockSpec(memory_space=pltpu.HBM)] * 15,
        out_specs=pl.BlockSpec(memory_space=pltpu.VMEM),
        scratch_shapes=[
            *[smem(x) for x in smalls], vmem(blocks, cells), vmem(n_if, cells),
            vmem(*whole), vmem(*whole), vmem(*whole), vmem(3, *whole), vmem(local, nv, nv, blocks, cells),
            vmem(blocks, cells), vmem(*whole), vmem(SWEEPS, *whole), vmem(*whole), vmem(SWEEPS, spare, *whole), vmem(half, *whole),
            vmem(SWEEPS, spare, *whole), vmem(SWEEPS, half, *whole), vmem(SWEEPS, *add), vmem(SWEEPS, spare, *add),
            vmem(n_mesh, slots, local * nv, cells), vmem(n_mesh, slots, local * nv, cells),
            vmem(SWEEPS, n_mesh, slots, local * nv, cells),
            vmem(n_mesh, n_if, total, nv, cells), vmem(n_mesh, n_if, total, nv, cells),
            vmem(SWEEPS, n_if, total, nv, cells),
            dma((4,)), dma((11,)),
            dma((SWEEPS, chunks)), dma((SWEEPS, spare, chunks)),
            dma((SWEEPS, half, chunks)), dma((SWEEPS, half, chunks)),
            dma((SWEEPS, spare, chunks)), dma((SWEEPS, chunks)),
            dma((SWEEPS, spare)), dma((SWEEPS,)),
            dma((SWEEPS, n_mesh)), dma((SWEEPS, n_mesh)), dma((SWEEPS, n_mesh)), dma((SWEEPS, n_mesh)),
            dma((half, chunks)), dma((chunks,)), pltpu.SemaphoreType.REGULAR,
        ],
        compiler_params=pltpu.CompilerParams(
            collective_id=0, has_side_effects=True, vmem_limit_bytes=VMEM_LIMIT
        ),
        name="smooth",
    )
    operands = (*smalls, state, right_side, couplings, jac_corr, spec_scale, iface_coef)
    updated = call(*(pltpu.with_memory_space_constraint(x, pltpu.HBM) for x in operands))
    least = np.full((nv, 1, 1), -np.inf, np.float32)
    least[-1] = 0.0
    return jnp.maximum(updated, least)


def solution(mesh):
    return jax.shard_map(
        functools.partial(per_device, mesh.shape["inst"], mesh.shape["mesh"]),
        mesh=mesh,
        in_specs=(
            P("inst", None, "mesh", None),
            P("inst", None, "mesh", None),
            P(None, "inst", None, "mesh", None),
            P("inst", None, None, "mesh", None),
            P("mesh", None),
            P("mesh"),
            P("mesh", None),
            P("mesh"),
            P("mesh", None),
            P("mesh", None),
            P("mesh", None),
            P("mesh"),
        ),
        out_specs=P("inst", None, "mesh", None),
        check_vma=False,
    )
```

```python
import functools

import jax
import jax.numpy as jnp
import numpy as np
from jax import lax
from jax.experimental import pallas as pl
from jax.experimental.pallas import tpu as pltpu
from jax.sharding import PartitionSpec as P

SWEEPS = 2
ROWS = 8
AHEAD = 3
FORWARD = 3
LATE = 2
GAP = 3
LAG = 2
SUMMED = 7
VMEM_LIMIT = 40 * 2**20
MESH_ID = pl.DeviceIdType.MESH


def spectral_matrix(length):
    offsets = np.arange(length)[:, None] - np.arange(length)[None, :]
    parity = 1.0 - 2.0 * (offsets % 2)
    angles = np.pi * offsets / length
    on_diag = offsets == 0
    sine = np.where(on_diag, 1.0, np.sin(angles))
    first = np.where(on_diag, 0.0, 0.5 * parity * np.cos(angles) / sine)
    second = np.where(on_diag, -(length * length + 2.0) / 12.0, -0.5 * parity / (sine * sine))
    return (first - 0.1 * second).astype(np.float32)


def hub_tables(n_inst, local):
    half, total = n_inst // 2, n_inst * local
    matrix = spectral_matrix(total)
    coefs, rows_abs, place = [], [], []
    for side in range(2):
        low, high = list(range(half - 1)), list(range(half + 1, n_inst))
        devs = [half - 1] + low + [half] + high if side == 0 else [half] + high + [half - 1] + low
        cols = np.array([d * local + i for d in devs for i in range(local)])
        rows = cols[: half * local]
        coefs.append(matrix[cols][:, cols].reshape(-1))
        rows_abs.append(rows)
        inverse = np.zeros(total, np.int32)
        inverse[cols] = np.arange(total)
        place.append(inverse)
    return np.stack(coefs), np.stack(rows_abs).astype(np.int32), np.stack(place)


def kernel(
    n_inst, n_mesh, dims,
    coef_in, rows_in, place_in, row_in, send_in, recv_in, donor_in, weight_in, phase_in,
    state, right_side, couplings, jac_corr, scale_in, iface_in,
    out,
    coef, rows_abs, place, row_id, send_index, recv_slot, donor_index, donor_weight, phase_shift, spec_scale, iface_coef,
    field0, field1, rhs, coup, jac, freq, halo, specin, specfar, specout, farout, raw_leaf, raw_other, iadd, iadd_out,
    inc0, inc1, hsend, pool0, pool1, fsend,
    load_sem, small_sem, s_leaf, r_leaf, s_other, r_other, s_spec, r_spec, s_iadd, r_iadd, s_halo, r_halo, s_face, r_face, s_far, r_far, ready,
):
    local, nv, blocks, cells, n_if, slots = dims
    half = n_inst // 2
    leaves = half - 1
    total = n_inst * local
    chunks = blocks // ROWS
    mid = chunks // 2
    me, my = lax.axis_index("inst"), lax.axis_index("mesh")
    side = me // half
    hub, other_hub = half - 1 + side, half - side
    leaf_at = me - side * (half + 1)
    fields, sent = (field0, field1, out), (state, field1)
    inc, pool = (inc0, inc1), (pool0, pool1)

    loads = [
        pltpu.make_async_copy(src, dst, load_sem.at[i])
        for i, (src, dst) in enumerate(
            ((state, field0), (right_side, rhs), (couplings, coup), (jac_corr, jac))
        )
    ]
    smalls = [
        pltpu.make_async_copy(src, dst, small_sem.at[i])
        for i, (src, dst) in enumerate(
            (
                (coef_in, coef), (rows_in, rows_abs), (place_in, place), (row_in, row_id), (send_in, send_index),
                (recv_in, recv_slot), (donor_in, donor_index), (weight_in, donor_weight), (phase_in, phase_shift),
                (scale_in, spec_scale), (iface_in, iface_coef),
            )
        )
    ]
    loads[0].start()
    for copy in smalls:
        copy.start()

    barrier = pltpu.get_barrier_semaphore()
    first_leaf = side * (half + 1)

    def greet(**where):
        pl.semaphore_signal(barrier, inc=1, device_id=where, device_id_type=MESH_ID)

    @pl.when(me == hub)
    def _():
        greet(inst=other_hub)
        for dev in range(n_mesh):
            greet(inst=first_leaf, mesh=dev)
        for i in range(1, leaves):
            greet(inst=first_leaf + i)

    @pl.when(me != hub)
    def _():
        for off in range(1, n_mesh):
            greet(mesh=lax.rem(my + off, n_mesh))

    greetings = jnp.where(leaf_at == 0, 2 * n_mesh - 1, n_mesh)
    pl.semaphore_wait(barrier, jnp.where(me == hub, 1, greetings))

    first_order = list(range(chunks))
    turn = min(LATE, chunks - 1)
    second_order = list(range(1, turn + 1)) + [0] + list(range(turn + 1, chunks))
    seq = [(0, c) for c in first_order] + [(1, c) for c in second_order]

    def part(ref, c):
        return ref.at[:, :, pl.ds(c * ROWS, ROWS), :]

    def remote(src, dst, send, recv, axis, dev):
        return pltpu.make_async_remote_copy(
            src_ref=src, dst_ref=dst, send_sem=send, recv_sem=recv,
            device_id={axis: dev}, device_id_type=MESH_ID,
        )

    def leaf_copy(s, c, i):
        return remote(
            part(sent[s], c), part(raw_leaf.at[s, i], c), s_leaf.at[s, c], r_leaf.at[s, i, c], "inst", hub
        )

    def own_copy(s, c):
        return remote(
            part(sent[s], c), part(raw_other.at[s, 0], c),
            s_other.at[s, 0, c], r_other.at[s, 0, c], "inst", other_hub,
        )

    def forward_copy(s, c, i):
        return remote(
            part(raw_leaf.at[s, i], c), part(raw_other.at[s, i + 1], c),
            s_other.at[s, i + 1, c], r_other.at[s, i + 1, c], "inst", other_hub,
        )

    def spec_copy(s, c, i):
        return remote(
            part(specout.at[s, i], c), part(specin.at[s], c),
            s_spec.at[s, i, c], r_spec.at[s, c], "inst", i + side * (half + 1),
        )

    def far_copy(c, k):
        dev = other_hub if k == 0 else k - 1 + (1 - side) * (half + 1)
        return remote(part(farout.at[k], c), part(specfar, c), s_far.at[k, c], r_far.at[c], "inst", dev)

    def iadd_copy(s, i):
        return remote(
            iadd_out.at[s, i], iadd.at[s], s_iadd.at[s, i], r_iadd.at[s], "inst", i + side * (half + 1)
        )

    def halo_copy(s, off):
        dev = lax.rem(my + off, n_mesh)
        return remote(hsend.at[s, dev], inc[s].at[my], s_halo.at[s, off], r_halo.at[s, off], "mesh", dev)

    def face_copy(s, off):
        dev = lax.rem(my + off, n_mesh)
        return remote(fsend.at[s], pool[s].at[my], s_face.at[s, off], r_face.at[s, off], "mesh", dev)

    def send_halo(s):
        def stage(d, carry):
            for k in range(slots):
                row = send_index[k, d]
                flat = fields[s].reshape(local * nv * blocks, cells)
                hsend[s, d, k] = flat[pl.ds(row, local * nv, stride=blocks), :]
            return carry

        lax.fori_loop(0, n_mesh, stage, 0)
        for off in range(1, n_mesh):
            halo_copy(s, off).start()
        for k in range(slots):
            inc[s][my, k] = hsend[s, my, k]

    def take_halo(s):
        for off in range(1, n_mesh):
            halo_copy(s, off).wait_recv()

    def expand_halo(s, c):
        flat = halo.reshape(local * nv * blocks, cells)
        for b in range(c * ROWS, c * ROWS + ROWS):
            slot = recv_slot[b]
            flat[pl.ds(b, local * nv, stride=blocks), :] = inc[s][slot // slots, slot % slots]

    def sources(s):
        refs = [(fields[s], n) for n in range(local)]
        refs += [(raw_leaf.at[s, i], n) for i in range(leaves) for n in range(local)]
        refs += [(raw_other.at[s, i], n) for i in range(half) for n in range(local)]
        return refs

    def spectral(s, row, v, rows, cols=total):
        acc = None
        for col, (ref, n) in enumerate(sources(s)[:cols]):
            term = coef[side, row * total + col] * ref[n, v, rows, :]
            acc = term if acc is None else acc + term
        return acc

    def update(s, c, is_hub, stage=None):
        field, target = fields[s], fields[s + 1]
        rows = pl.ds(c * ROWS, ROWS)
        lane = lax.broadcasted_iota(jnp.int32, (ROWS, cells), 1)

        def gather(n, v):
            if stage == 1:
                return rhs[n, v, rows, :] - freq[rows, :] * specfar[n, v, rows, :]
            x = field[n, v, rows, :]
            below = jnp.where(lane == 0, 0.0, pltpu.roll(x, 1, 1))
            above = jnp.where(lane == cells - 1, 0.0, pltpu.roll(x, cells - 1, 1))
            spec = spectral(s, n, v, rows) if is_hub and stage is None else specin[s, n, v, rows, :]
            value = rhs[n, v, rows, :] + coup[0, n, v, rows, :] * below + coup[1, n, v, rows, :] * above
            value = value + coup[2, n, v, rows, :] * halo[n, v, rows, :] - freq[rows, :] * spec
            if c == 0:
                value = value + iadd[s, n, v]
            return value

        def one(n, carry):
            if stage == 0:
                for v in range(nv):
                    rhs[n, v, rows, :] = gather(n, v)
                return carry
            parts = [gather(n, v) for v in range(nv)]
            for v in range(nv):
                acc = 0.35 * parts[v]
                for w in range(nv):
                    acc = acc + jac[n, v, w, rows, :] * parts[w]
                if v == nv - 1 and s + 1 < SWEEPS:
                    acc = jnp.maximum(acc, 0.0)
                target[n, v, rows, :] = acc
            return carry

        lax.fori_loop(0, local, one, 0)

    def send_faces(s):
        for col, (ref, n) in enumerate(sources(s)):
            for j in range(n_if):
                for v in range(nv):
                    fsend[s, j, col, pl.ds(v, 1), :] = ref[n, v, pl.ds(j, 1), :]
        for off in range(1, n_mesh):
            face_copy(s, off).start()
        for j in range(n_if):
            pool[s][my, j] = fsend[s, j]

    def mix_faces(s):
        for off in range(1, n_mesh):
            face_copy(s, off).wait_recv()
        for j in range(n_if):
            first, second = donor_index[j, 0], donor_index[j, 1]
            scale = iface_coef[pl.ds(j, 1), :]

            def one(row, carry):
                at = place[side, lax.rem(rows_abs[side, row] + phase_shift[j], total)]
                mixed = donor_weight[j, 0] * pool[s][first // n_if, first % n_if, at]
                mixed = mixed + donor_weight[j, 1] * pool[s][second // n_if, second % n_if, at]
                return mixed * scale

            for n in range(local):
                value = one(n, 0)
                for v in range(nv):
                    iadd[s, n, v, pl.ds(j, 1), :] = value[v : v + 1]
            for i in range(leaves):
                for n in range(local):
                    value = one((i + 1) * local + n, 0)
                    for v in range(nv):
                        iadd_out[s, i, n, v, pl.ds(j, 1), :] = value[v : v + 1]
        for i in range(leaves):
            iadd_copy(s, i).start()

    def prepare():
        for copy in loads[1:]:
            copy.wait()

        def one(b, carry):
            freq[pl.ds(b, 1), :] = spec_scale[pl.ds(b, 1), :] * (1.0 + 0.5 * row_id[b].astype(jnp.float32))
            return carry

        lax.fori_loop(0, blocks, one, 0)

    def run(is_hub):
        last = SWEEPS - 1

        def summed(s, c):
            return s == last and c in second_order[-SUMMED:] and c > 0

        def get(s, c):
            if not is_hub:
                spec_copy(s, c, 0).wait_recv()
                return
            own_copy(s, c).wait_recv()
            for i in range(leaves):
                forward_copy(s, c, i).wait_recv()
            for i in range(leaves):
                sums(s, c, i + 1, total, specout.at[s, i])
                spec_copy(s, c, i).start()
            if c == 0:
                send_faces(s)

        def sums(s, c, block, cols, target):
            rows = pl.ds(c * ROWS, ROWS)

            def one(n, carry):
                for v in range(nv):
                    target[n, v, rows, :] = spectral(s, block * local + n, v, rows, cols)
                return carry

            lax.fori_loop(0, local, one, 0)

        def near_sums(c):
            if not is_hub or not summed(last, c):
                return
            for i in range(leaves):
                leaf_copy(last, c, i).wait_recv()
            for i in range(leaves):
                sums(last, c, i + 1, half * local, specout.at[last, i])
                spec_copy(last, c, i).start()
            sums(last, c, 0, half * local, specin.at[last])

        def far_sums(c):
            for k in range(1, half + 1):
                k = k % half
                sums(last, c, half + k, half * local, farout.at[k])
                far_copy(c, k).start()

        def own(j):
            if is_hub and j < len(seq) and not summed(*seq[j]):
                own_copy(*seq[j]).start()

        def forward(j):
            if not is_hub or j >= len(seq):
                return
            if summed(*seq[j]):
                far_sums(seq[j][1])
                return
            for i in range(leaves):
                leaf_copy(*seq[j], i).wait_recv()
                forward_copy(*seq[j], i).start()

        def smooth(s, c):
            if c == 0:
                if is_hub:
                    mix_faces(s)
                else:
                    iadd_copy(s, 0).wait_recv()
            expand_halo(s, c)
            update(s, c, is_hub)
            if s + 1 < SWEEPS and not is_hub:
                leaf_copy(s + 1, c, leaf_at).start()

        def finish(c):
            if not is_hub:
                spec_copy(last, c, 0).wait_recv()
            expand_halo(last, c)
            update(last, c, is_hub, 0)
            far_copy(c, 0).wait_recv()
            update(last, c, is_hub, 1)

        if is_hub:
            for j in range(AHEAD):
                own(j)
        else:
            pl.semaphore_signal(ready, inc=1, device_id={"inst": hub}, device_id_type=MESH_ID)
            for c in first_order:
                leaf_copy(0, c, leaf_at).start()
        for copy in loads[1:]:
            copy.start()
        loads[0].wait()
        for copy in smalls:
            copy.wait()
        if is_hub:
            for s in range(SWEEPS):
                iadd[s] = jnp.zeros_like(iadd[s])
                iadd_out[s] = jnp.zeros_like(iadd_out[s])
            pl.semaphore_wait(ready, leaves)
        send_halo(0)
        for j in range(FORWARD):
            forward(j)
        for j, c in enumerate(first_order):
            own(j + AHEAD)
            forward(j + FORWARD)
            get(0, c)
            if j == 0:
                prepare()
                take_halo(0)
            if c > 0:
                smooth(0, c)
            if j == mid:
                smooth(0, 0)
            if j >= LAG:
                near_sums(j - LAG)
        send_halo(1)
        waiting = []
        for p, c in enumerate(second_order):
            if p < LAG:
                near_sums(chunks - LAG + p)
            own(chunks + p + AHEAD)
            forward(chunks + p + FORWARD)
            if not summed(1, c):
                get(1, c)
            if c > 0:
                waiting.append(c)
            if p == 2:
                take_halo(1)
            if p >= 2:
                for w in waiting:
                    (finish if summed(1, w) else functools.partial(smooth, 1))(w)
                waiting = []
            if p == min(turn + GAP, chunks - 1):
                smooth(1, 0)
        for s, c in seq:
            if is_hub:
                if summed(s, c):
                    for k in range(half):
                        far_copy(c, k).wait_send()
                else:
                    own_copy(s, c).wait_send()
                    for i in range(leaves):
                        forward_copy(s, c, i).wait_send()
                for i in range(leaves):
                    spec_copy(s, c, i).wait_send()
            else:
                leaf_copy(s, c, leaf_at).wait_send()
        for s in range(SWEEPS):
            for off in range(1, n_mesh):
                halo_copy(s, off).wait_send()
                if is_hub:
                    face_copy(s, off).wait_send()
            if is_hub:
                for i in range(leaves):
                    iadd_copy(s, i).wait_send()

    @pl.when(me == hub)
    def _():
        run(True)

    @pl.when(me != hub)
    def _():
        run(False)


def per_device(
    n_inst, n_mesh,
    state, right_side, couplings, jac_corr, spec_scale, row_id, send_index, recv_slot,
    iface_coef, donor_index, donor_weight, phase_shift,
):
    local, nv, blocks, cells = state.shape
    n_if, slots = iface_coef.shape[0], send_index.shape[1]
    half, total = n_inst // 2, n_inst * local
    spare = max(half - 1, 1)
    chunks = blocks // ROWS
    tables = [jnp.asarray(t) for t in hub_tables(n_inst, local)]
    f32 = jnp.float32
    dma = pltpu.SemaphoreType.DMA
    whole = (local, nv, blocks, cells)
    add = (local, nv, ROWS, cells)
    vmem = lambda *shape: pltpu.VMEM(shape, f32)
    smem = lambda x: pltpu.SMEM(x.shape, x.dtype)
    smalls = [*tables, row_id, send_index.T, recv_slot, donor_index, donor_weight, phase_shift]
    call = pl.pallas_call(
        functools.partial(kernel, n_inst, n_mesh, (local, nv, blocks, cells, n_if, slots)),
        out_shape=pltpu.VMEM(whole, f32),
        in_specs=[pl.BlockSpec(memory_space=pltpu.HBM)] * 15,
        out_specs=pl.BlockSpec(memory_space=pltpu.VMEM),
        scratch_shapes=[
            *[smem(x) for x in smalls], vmem(blocks, cells), vmem(n_if, cells),
            vmem(*whole), vmem(*whole), vmem(*whole), vmem(3, *whole), vmem(local, nv, nv, blocks, cells),
            vmem(blocks, cells), vmem(*whole), vmem(SWEEPS, *whole), vmem(*whole), vmem(SWEEPS, spare, *whole), vmem(half, *whole),
            vmem(SWEEPS, spare, *whole), vmem(SWEEPS, half, *whole), vmem(SWEEPS, *add), vmem(SWEEPS, spare, *add),
            vmem(n_mesh, slots, local * nv, cells), vmem(n_mesh, slots, local * nv, cells),
            vmem(SWEEPS, n_mesh, slots, local * nv, cells),
            vmem(n_mesh, n_if, total, nv, cells), vmem(n_mesh, n_if, total, nv, cells),
            vmem(SWEEPS, n_if, total, nv, cells),
            dma((4,)), dma((11,)),
            dma((SWEEPS, chunks)), dma((SWEEPS, spare, chunks)),
            dma((SWEEPS, half, chunks)), dma((SWEEPS, half, chunks)),
            dma((SWEEPS, spare, chunks)), dma((SWEEPS, chunks)),
            dma((SWEEPS, spare)), dma((SWEEPS,)),
            dma((SWEEPS, n_mesh)), dma((SWEEPS, n_mesh)), dma((SWEEPS, n_mesh)), dma((SWEEPS, n_mesh)),
            dma((half, chunks)), dma((chunks,)), pltpu.SemaphoreType.REGULAR,
        ],
        compiler_params=pltpu.CompilerParams(
            collective_id=0, has_side_effects=True, vmem_limit_bytes=VMEM_LIMIT
        ),
        name="smooth",
    )
    operands = (*smalls, state, right_side, couplings, jac_corr, spec_scale, iface_coef)
    updated = call(*(pltpu.with_memory_space_constraint(x, pltpu.HBM) for x in operands))
    least = np.full((nv, 1, 1), -np.inf, np.float32)
    least[-1] = 0.0
    return jnp.maximum(updated, least)


def solution(mesh):
    return jax.shard_map(
        functools.partial(per_device, mesh.shape["inst"], mesh.shape["mesh"]),
        mesh=mesh,
        in_specs=(
            P("inst", None, "mesh", None),
            P("inst", None, "mesh", None),
            P(None, "inst", None, "mesh", None),
            P("inst", None, None, "mesh", None),
            P("mesh", None),
            P("mesh"),
            P("mesh", None),
            P("mesh"),
            P("mesh", None),
            P("mesh", None),
            P("mesh", None),
            P("mesh"),
        ),
        out_specs=P("inst", None, "mesh", None),
        check_vma=False,
    )
```

```python
import functools

import jax
import jax.numpy as jnp
import numpy as np
from jax import lax
from jax.experimental import pallas as pl
from jax.experimental.pallas import tpu as pltpu
from jax.sharding import PartitionSpec as P

SWEEPS = 2
ROWS = 8
AHEAD = 3
FORWARD = 3
LATE = 2
GAP = 3
LAG = 2
SUMMED = 5
VMEM_LIMIT = 40 * 2**20
MESH_ID = pl.DeviceIdType.MESH


def spectral_matrix(length):
    offsets = np.arange(length)[:, None] - np.arange(length)[None, :]
    parity = 1.0 - 2.0 * (offsets % 2)
    angles = np.pi * offsets / length
    on_diag = offsets == 0
    sine = np.where(on_diag, 1.0, np.sin(angles))
    first = np.where(on_diag, 0.0, 0.5 * parity * np.cos(angles) / sine)
    second = np.where(on_diag, -(length * length + 2.0) / 12.0, -0.5 * parity / (sine * sine))
    return (first - 0.1 * second).astype(np.float32)


def hub_tables(n_inst, local):
    half, total = n_inst // 2, n_inst * local
    matrix = spectral_matrix(total)
    coefs, rows_abs, place = [], [], []
    for side in range(2):
        low, high = list(range(half - 1)), list(range(half + 1, n_inst))
        devs = [half - 1] + low + [half] + high if side == 0 else [half] + high + [half - 1] + low
        cols = np.array([d * local + i for d in devs for i in range(local)])
        rows = cols[: half * local]
        coefs.append(matrix[cols][:, cols].reshape(-1))
        rows_abs.append(rows)
        inverse = np.zeros(total, np.int32)
        inverse[cols] = np.arange(total)
        place.append(inverse)
    return np.stack(coefs), np.stack(rows_abs).astype(np.int32), np.stack(place)


def kernel(
    n_inst, n_mesh, dims,
    coef_in, rows_in, place_in, row_in, send_in, recv_in, donor_in, weight_in, phase_in,
    state, right_side, couplings, jac_corr, scale_in, iface_in,
    out,
    coef, rows_abs, place, row_id, send_index, recv_slot, donor_index, donor_weight, phase_shift, spec_scale, iface_coef,
    field0, field1, rhs, coup, jac, freq, halo, specin, specfar, specout, farout, raw_leaf, raw_other, iadd, iadd_out,
    inc0, inc1, hsend, pool0, pool1, fsend,
    first_sem, load_sem, small_sem, s_leaf, r_leaf, s_other, r_other, s_spec, r_spec, s_iadd, r_iadd, s_halo, r_halo, s_face, r_face, s_far, r_far, ready,
):
    local, nv, blocks, cells, n_if, slots = dims
    half = n_inst // 2
    leaves = half - 1
    total = n_inst * local
    chunks = blocks // ROWS
    mid = chunks // 2
    me, my = lax.axis_index("inst"), lax.axis_index("mesh")
    side = me // half
    hub, other_hub = half - 1 + side, half - side
    leaf_at = me - side * (half + 1)
    fields = (field0, field1, out)
    inc, pool = (inc0, inc1), (pool0, pool1)

    firsts = [
        pltpu.make_async_copy(state.at[:, :, pl.ds(c * ROWS, ROWS), :], field0.at[c], first_sem.at[c]) for c in range(chunks)
    ]
    loads = [
        pltpu.make_async_copy(src, dst, load_sem.at[i])
        for i, (src, dst) in enumerate(((right_side, rhs), (couplings, coup), (jac_corr, jac)))
    ]
    smalls = [
        pltpu.make_async_copy(src, dst, small_sem.at[i])
        for i, (src, dst) in enumerate(
            (
                (coef_in, coef), (rows_in, rows_abs), (place_in, place), (row_in, row_id), (send_in, send_index),
                (recv_in, recv_slot), (donor_in, donor_index), (weight_in, donor_weight), (phase_in, phase_shift),
                (scale_in, spec_scale), (iface_in, iface_coef),
            )
        )
    ]
    for copy in firsts:
        copy.start()
    for copy in smalls:
        copy.start()

    barrier = pltpu.get_barrier_semaphore()
    first_leaf = side * (half + 1)

    def greet(**where):
        pl.semaphore_signal(barrier, inc=1, device_id=where, device_id_type=MESH_ID)

    @pl.when(me == hub)
    def _():
        greet(inst=other_hub)
        for dev in range(n_mesh):
            greet(inst=first_leaf, mesh=dev)
        for i in range(1, leaves):
            greet(inst=first_leaf + i)

    @pl.when(me != hub)
    def _():
        for off in range(1, n_mesh):
            greet(mesh=lax.rem(my + off, n_mesh))

    greetings = jnp.where(leaf_at == 0, 2 * n_mesh - 1, n_mesh)
    pl.semaphore_wait(barrier, jnp.where(me == hub, 1, greetings))

    first_order = list(range(chunks))
    turn = min(LATE, chunks - 1)
    second_order = list(range(1, turn + 1)) + [0] + list(range(turn + 1, chunks))
    seq = [(0, c) for c in first_order] + [(1, c) for c in second_order]

    def part(ref, c):
        return ref.at[c]

    def remote(src, dst, send, recv, axis, dev):
        return pltpu.make_async_remote_copy(
            src_ref=src, dst_ref=dst, send_sem=send, recv_sem=recv,
            device_id={axis: dev}, device_id_type=MESH_ID,
        )

    def leaf_copy(s, c, i):
        return remote(
            part(fields[s], c), part(raw_leaf.at[s, i], c), s_leaf.at[s, c], r_leaf.at[s, i, c], "inst", hub
        )

    def own_copy(s, c):
        early = s == 0 and c < AHEAD
        return remote(
            state.at[:, :, pl.ds(c * ROWS, ROWS), :] if early else part(fields[s], c), part(raw_other.at[s, 0], c),
            s_other.at[s, 0, c], r_other.at[s, 0, c], "inst", other_hub,
        )

    def forward_copy(s, c, i):
        return remote(
            part(raw_leaf.at[s, i], c), part(raw_other.at[s, i + 1], c),
            s_other.at[s, i + 1, c], r_other.at[s, i + 1, c], "inst", other_hub,
        )

    def spec_copy(s, c, i):
        return remote(
            part(specout.at[s, i], c), part(specin.at[s], c),
            s_spec.at[s, i, c], r_spec.at[s, c], "inst", i + side * (half + 1),
        )

    def far_copy(c, k):
        dev = other_hub if k == 0 else k - 1 + (1 - side) * (half + 1)
        return remote(part(farout.at[k], c), part(specfar, c), s_far.at[k, c], r_far.at[c], "inst", dev)

    def iadd_copy(s, i):
        return remote(
            iadd_out.at[s, i], iadd.at[s], s_iadd.at[s, i], r_iadd.at[s], "inst", i + side * (half + 1)
        )

    def halo_copy(s, off):
        dev = lax.rem(my + off, n_mesh)
        return remote(hsend.at[s, dev], inc[s].at[my], s_halo.at[s, off], r_halo.at[s, off], "mesh", dev)

    def face_copy(s, off):
        dev = lax.rem(my + off, n_mesh)
        return remote(fsend.at[s], pool[s].at[my], s_face.at[s, off], r_face.at[s, off], "mesh", dev)

    def send_halo(s):
        def stage(d, carry):
            for k in range(slots):
                row = send_index[k, d]
                at = row // ROWS * (local * nv * ROWS) + row % ROWS
                flat = fields[s].reshape(local * nv * blocks, cells)
                hsend[s, d, k] = flat[pl.ds(at, local * nv, stride=ROWS), :]
            return carry

        lax.fori_loop(0, n_mesh, stage, 0)
        for off in range(1, n_mesh):
            halo_copy(s, off).start()
        for k in range(slots):
            inc[s][my, k] = hsend[s, my, k]

    def take_halo(s):
        for off in range(1, n_mesh):
            halo_copy(s, off).wait_recv()

    def expand_halo(s, c):
        flat = halo.reshape(local * nv * blocks, cells)
        for b in range(c * ROWS, c * ROWS + ROWS):
            slot = recv_slot[b]
            flat[pl.ds(b, local * nv, stride=blocks), :] = inc[s][slot // slots, slot % slots]

    def sources(s):
        refs = [(fields[s], n) for n in range(local)]
        refs += [(raw_leaf.at[s, i], n) for i in range(leaves) for n in range(local)]
        refs += [(raw_other.at[s, i], n) for i in range(half) for n in range(local)]
        return refs

    def spectral(s, row, v, c, cols=total):
        acc = None
        for col, (ref, n) in enumerate(sources(s)[:cols]):
            term = coef[side, row * total + col] * ref[c, n, v]
            acc = term if acc is None else acc + term
        return acc

    def update(s, c, is_hub, stage=None):
        field, target = fields[s], fields[s + 1]
        rows = pl.ds(c * ROWS, ROWS)
        lane = lax.broadcasted_iota(jnp.int32, (ROWS, cells), 1)

        def gather(n, v):
            if stage == 1:
                return rhs[n, v, rows, :] - freq[rows, :] * specfar[c, n, v]
            x = field[c, n, v]
            below = jnp.where(lane == 0, 0.0, pltpu.roll(x, 1, 1))
            above = jnp.where(lane == cells - 1, 0.0, pltpu.roll(x, cells - 1, 1))
            spec = spectral(s, n, v, c) if is_hub and stage is None else specin[s, c, n, v]
            value = rhs[n, v, rows, :] + coup[0, n, v, rows, :] * below + coup[1, n, v, rows, :] * above
            value = value + coup[2, n, v, rows, :] * halo[n, v, rows, :] - freq[rows, :] * spec
            if c == 0:
                value = value + iadd[s, n, v]
            return value

        def one(n, carry):
            if stage == 0:
                for v in range(nv):
                    rhs[n, v, rows, :] = gather(n, v)
                return carry
            parts = [gather(n, v) for v in range(nv)]
            for v in range(nv):
                acc = 0.35 * parts[v]
                for w in range(nv):
                    acc = acc + jac[n, v, w, rows, :] * parts[w]
                if v == nv - 1 and s + 1 < SWEEPS:
                    acc = jnp.maximum(acc, 0.0)
                if s + 1 < SWEEPS:
                    target[c, n, v] = acc
                else:
                    target[n, v, rows, :] = acc
            return carry

        lax.fori_loop(0, local, one, 0)

    def send_faces(s):
        for col, (ref, n) in enumerate(sources(s)):
            for j in range(n_if):
                for v in range(nv):
                    fsend[s, j, col, pl.ds(v, 1), :] = ref[0, n, v, pl.ds(j, 1), :]
        for off in range(1, n_mesh):
            face_copy(s, off).start()
        for j in range(n_if):
            pool[s][my, j] = fsend[s, j]

    def mix_faces(s):
        for off in range(1, n_mesh):
            face_copy(s, off).wait_recv()
        for j in range(n_if):
            first, second = donor_index[j, 0], donor_index[j, 1]
            scale = iface_coef[pl.ds(j, 1), :]

            def one(row, carry):
                at = place[side, lax.rem(rows_abs[side, row] + phase_shift[j], total)]
                mixed = donor_weight[j, 0] * pool[s][first // n_if, first % n_if, at]
                mixed = mixed + donor_weight[j, 1] * pool[s][second // n_if, second % n_if, at]
                return mixed * scale

            for n in range(local):
                value = one(n, 0)
                for v in range(nv):
                    iadd[s, n, v, pl.ds(j, 1), :] = value[v : v + 1]
            for i in range(leaves):
                for n in range(local):
                    value = one((i + 1) * local + n, 0)
                    for v in range(nv):
                        iadd_out[s, i, n, v, pl.ds(j, 1), :] = value[v : v + 1]
        for i in range(leaves):
            iadd_copy(s, i).start()

    def prepare():
        for copy in loads:
            copy.wait()

        def one(b, carry):
            freq[pl.ds(b, 1), :] = spec_scale[pl.ds(b, 1), :] * (1.0 + 0.5 * row_id[b].astype(jnp.float32))
            return carry

        lax.fori_loop(0, blocks, one, 0)

    def run(is_hub):
        last = SWEEPS - 1
        first_core = lax.rem(my, 2) == 0

        def summed(s, c):
            return s == last and c in second_order[-SUMMED:] and c > 0

        def get(s, c):
            if not is_hub:
                spec_copy(s, c, 0).wait_recv()
                return
            own_copy(s, c).wait_recv()
            for i in range(leaves):
                forward_copy(s, c, i).wait_recv()
            for i in range(leaves):
                sums(s, c, i + 1, total, specout.at[s, i])
                spec_copy(s, c, i).start()
            if c == 0:
                send_faces(s)

        def sums(s, c, block, cols, target):
            def one(n, carry):
                for v in range(nv):
                    target[c, n, v] = spectral(s, block * local + n, v, c, cols)
                return carry

            lax.fori_loop(0, local, one, 0)

        def near_sums(c):
            if not is_hub or not summed(last, c):
                return
            for i in range(leaves):
                leaf_copy(last, c, i).wait_recv()
            for i in range(leaves):
                sums(last, c, i + 1, half * local, specout.at[last, i])
                spec_copy(last, c, i).start()
            sums(last, c, 0, half * local, specin.at[last])

        def far_sums(c, which):
            for k in which:
                sums(last, c, half + k, half * local, farout.at[k])
                far_copy(c, k).start()

        def own(j):
            if is_hub and j < len(seq) and not summed(*seq[j]):
                own_copy(*seq[j]).start()

        def forward(j):
            if not is_hub or j >= len(seq):
                return
            if summed(*seq[j]):
                if j < len(seq) - 1:
                    far_sums(seq[j][1], range(1, half))
                else:
                    pl.when(first_core)(lambda: far_sums(seq[j][1], [*range(1, half), 0]))
                if j < len(seq) - 1:
                    far_sums(seq[j][1], [0])
                return
            for i in range(leaves):
                leaf_copy(*seq[j], i).wait_recv()
                forward_copy(*seq[j], i).start()

        def smooth(s, c):
            if c == 0:
                if is_hub:
                    mix_faces(s)
                else:
                    iadd_copy(s, 0).wait_recv()
            expand_halo(s, c)
            update(s, c, is_hub)
            if s + 1 < SWEEPS and not is_hub:
                leaf_copy(s + 1, c, leaf_at).start()

        def finish(c):
            if not is_hub:
                spec_copy(last, c, 0).wait_recv()
            expand_halo(last, c)
            update(last, c, is_hub, 0)
            far_copy(c, 0).wait_recv()
            update(last, c, is_hub, 1)

        if is_hub:
            for j in range(AHEAD):
                own(j)
        for copy in firsts:
            copy.wait()
        if not is_hub:
            pl.semaphore_signal(ready, inc=1, device_id={"inst": hub}, device_id_type=MESH_ID)
            for c in first_order:
                leaf_copy(0, c, leaf_at).start()
        for copy in loads:
            copy.start()
        for copy in smalls:
            copy.wait()
        if is_hub:
            for s in range(SWEEPS):
                iadd[s] = jnp.zeros_like(iadd[s])
                iadd_out[s] = jnp.zeros_like(iadd_out[s])
            pl.semaphore_wait(ready, leaves)
        send_halo(0)
        for j in range(FORWARD):
            forward(j)
        for j, c in enumerate(first_order):
            own(j + AHEAD)
            forward(j + FORWARD)
            get(0, c)
            if j == 0:
                prepare()
                take_halo(0)
            if c > 0:
                smooth(0, c)
            if j == mid:
                smooth(0, 0)
            if j >= LAG:
                near_sums(j - LAG)
        send_halo(1)
        waiting = []
        for p, c in enumerate(second_order):
            if p < LAG:
                near_sums(chunks - LAG + p)
            own(chunks + p + AHEAD)
            forward(chunks + p + FORWARD)
            if not summed(1, c):
                get(1, c)
            if c > 0:
                waiting.append(c)
            if p == 2:
                take_halo(1)
            if p == chunks - 1 and is_hub and summed(1, c):
                pl.when(jnp.logical_not(first_core))(lambda: far_sums(c, [*range(1, half), 0]))
            if p >= 2:
                for w in waiting:
                    (finish if summed(1, w) else functools.partial(smooth, 1))(w)
                waiting = []
            if p == min(turn + GAP, chunks - 1):
                smooth(1, 0)
        for s, c in seq:
            if is_hub:
                if summed(s, c):
                    for k in range(half):
                        far_copy(c, k).wait_send()
                else:
                    own_copy(s, c).wait_send()
                    for i in range(leaves):
                        forward_copy(s, c, i).wait_send()
                for i in range(leaves):
                    spec_copy(s, c, i).wait_send()
            else:
                leaf_copy(s, c, leaf_at).wait_send()
        for s in range(SWEEPS):
            for off in range(1, n_mesh):
                halo_copy(s, off).wait_send()
                if is_hub:
                    face_copy(s, off).wait_send()
            if is_hub:
                for i in range(leaves):
                    iadd_copy(s, i).wait_send()

    @pl.when(me == hub)
    def _():
        run(True)

    @pl.when(me != hub)
    def _():
        run(False)


def per_device(
    n_inst, n_mesh,
    state, right_side, couplings, jac_corr, spec_scale, row_id, send_index, recv_slot,
    iface_coef, donor_index, donor_weight, phase_shift,
):
    local, nv, blocks, cells = state.shape
    n_if, slots = iface_coef.shape[0], send_index.shape[1]
    half, total = n_inst // 2, n_inst * local
    spare = max(half - 1, 1)
    chunks = blocks // ROWS
    tables = [jnp.asarray(t) for t in hub_tables(n_inst, local)]
    f32 = jnp.float32
    dma = pltpu.SemaphoreType.DMA
    whole, cut = (local, nv, blocks, cells), (chunks, local, nv, ROWS, cells)
    add = (local, nv, ROWS, cells)
    vmem = lambda *shape: pltpu.VMEM(shape, f32)
    smem = lambda x: pltpu.SMEM(x.shape, x.dtype)
    smalls = [*tables, row_id, send_index.T, recv_slot, donor_index, donor_weight, phase_shift]
    call = pl.pallas_call(
        functools.partial(kernel, n_inst, n_mesh, (local, nv, blocks, cells, n_if, slots)),
        out_shape=pltpu.VMEM(whole, f32),
        in_specs=[pl.BlockSpec(memory_space=pltpu.HBM)] * 15,
        out_specs=pl.BlockSpec(memory_space=pltpu.VMEM),
        scratch_shapes=[
            *[smem(x) for x in smalls], vmem(blocks, cells), vmem(n_if, cells),
            vmem(*cut), vmem(*cut), vmem(*whole), vmem(3, *whole), vmem(local, nv, nv, blocks, cells),
            vmem(blocks, cells), vmem(*whole), vmem(SWEEPS, *cut), vmem(*cut), vmem(SWEEPS, spare, *cut), vmem(half, *cut),
            vmem(SWEEPS, spare, *cut), vmem(SWEEPS, half, *cut), vmem(SWEEPS, *add), vmem(SWEEPS, spare, *add),
            vmem(n_mesh, slots, local * nv, cells), vmem(n_mesh, slots, local * nv, cells),
            vmem(SWEEPS, n_mesh, slots, local * nv, cells),
            vmem(n_mesh, n_if, total, nv, cells), vmem(n_mesh, n_if, total, nv, cells),
            vmem(SWEEPS, n_if, total, nv, cells),
            dma((chunks,)), dma((3,)), dma((11,)),
            dma((SWEEPS, chunks)), dma((SWEEPS, spare, chunks)),
            dma((SWEEPS, half, chunks)), dma((SWEEPS, half, chunks)),
            dma((SWEEPS, spare, chunks)), dma((SWEEPS, chunks)),
            dma((SWEEPS, spare)), dma((SWEEPS,)),
            dma((SWEEPS, n_mesh)), dma((SWEEPS, n_mesh)), dma((SWEEPS, n_mesh)), dma((SWEEPS, n_mesh)),
            dma((half, chunks)), dma((chunks,)), pltpu.SemaphoreType.REGULAR,
        ],
        compiler_params=pltpu.CompilerParams(
            collective_id=0, has_side_effects=True, vmem_limit_bytes=VMEM_LIMIT
        ),
        name="smooth",
    )
    operands = (*smalls, state, right_side, couplings, jac_corr, spec_scale, iface_coef)
    updated = call(*(pltpu.with_memory_space_constraint(x, pltpu.HBM) for x in operands))
    least = np.full((nv, 1, 1), -np.inf, np.float32)
    least[-1] = 0.0
    return jnp.maximum(updated, least)


def solution(mesh):
    return jax.shard_map(
        functools.partial(per_device, mesh.shape["inst"], mesh.shape["mesh"]),
        mesh=mesh,
        in_specs=(
            P("inst", None, "mesh", None),
            P("inst", None, "mesh", None),
            P(None, "inst", None, "mesh", None),
            P("inst", None, None, "mesh", None),
            P("mesh", None),
            P("mesh"),
            P("mesh", None),
            P("mesh"),
            P("mesh", None),
            P("mesh", None),
            P("mesh", None),
            P("mesh"),
        ),
        out_specs=P("inst", None, "mesh", None),
        check_vma=False,
    )
```
